32 devices in a mesh: group: 2 (over y), tile: 16 (over z, x, core).
Axes of the slice: x: 2, y: 2, z: 4, core: 2. Of those that a mesh axis runs over, the one named last changes fastest.
Arguments:
- site_tensors: bfloat16 [16, 6, 2, 65536], P('tile', 'group'), may hold values from -6 to 6
- msg_in: float32 [16, 6, 4, 256], P('tile', 'group'), may hold values from -6 to 6
Outputs:
- new_tensors: bfloat16 [16, 6, 2, 65536], P('tile', 'group')
- messages: float32 [16, 6, 4, 256], P('tile', 'group')
The draws below stay inside these ranges and needn't reach their ends.
All inputs are finite; a program needn't handle non-finite values.
Results may differ from the reference program's by a relative error of at most 0.029.
The reference program's roundings to bfloat16 on the way count: a program that leaves them out, or rounds other values in their place, can miss the bound.
Values may be sent and summed in bfloat16 or wider, within the bound.
A program may use at most 256 MiB of HBM per device.

```python
import math
import jax
import jax.numpy as jnp
from jax import lax

D = 16
ITERS = 2
NS_STEPS = 6
COLS = 6
ROWS = 16


def steps_of(own_key, extent, split, low, largest):
    def one(position, parts):
        draws = jax.random.uniform(jax.random.fold_in(jax.random.fold_in(own_key, 6), position), (parts,), jnp.float32, low / len(split), largest / len(split))
        return jnp.repeat(jnp.exp(draws), extent[position] // parts).reshape((-1,) + (1,) * (len(extent) - position - 1))

    factor_of = one(*split[0])
    for cut in split[1:]:
        factor_of = factor_of * one(*cut)
    return factor_of


def centred(key, extent, deviation, bound, cuts=(), kind=jnp.bfloat16):
    array = jax.random.normal(key, extent, jnp.float32) * deviation
    if len(cuts) > 0:
        array = steps_of(key, extent, cuts, -0.22, 0.18) * array
    return jnp.clip(array, min=-bound, max=bound).astype(kind)


def setup_inputs(seed: int = 0) -> dict:
    keys = jax.random.split(jax.random.key(seed), 3)
    site_tensors = centred(keys[0], (ROWS, COLS, 2, D**4), 1.0, 6.0, ((0, 16), (1, 2)))
    msg_in = centred(keys[1], (ROWS, COLS, 4, D*D), 1.0, 6.0, ((0, 16), (1, 2)), jnp.float32)
    return dict(site_tensors=site_tensors, msg_in=msg_in)


epsilon = 1e-06
coupling_step = 0.5
field_step = 0.3
precise = lax.Precision.HIGHEST
apply_forms = ('nsuldr,nua->nsaldr', 'nsuldr,nla->nsuadr', 'nsuldr,nda->nsular', 'nsuldr,nra->nsulda')
gate_forms = ('nsuldr,nsua->nsaldr', 'nsuldr,nsla->nsuadr', 'nsuldr,nsda->nsular', 'nsuldr,nsra->nsulda')
pair_forms = ('nsuldr,nsvldr->nsuv', 'nsuldr,nsuvdr->nslv', 'nsuldr,nsulvr->nsdv', 'nsuldr,nsuldv->nsrv')

def contract(form, left_op, right_op):
    return jnp.einsum(form, left_op.astype(jnp.float32), right_op.astype(jnp.float32), precision=precise)

def outgoing(tensors, incoming):
    site_count = tensors.shape[0]
    site_block = tensors.reshape(site_count, 2, D, D, D, D)
    msg_bf = incoming.reshape(site_count, 4, D, D).astype(jnp.bfloat16)

    def apply_leg(tensor, leg_idx):
        return contract(apply_forms[leg_idx], tensor, msg_bf[:, leg_idx]).astype(jnp.bfloat16)
    upper_left = apply_leg(apply_leg(site_block, 0), 1)
    lower_right = apply_leg(apply_leg(site_block, 2), 3)
    kept = (apply_leg(lower_right, 1), apply_leg(lower_right, 0), apply_leg(upper_left, 3), apply_leg(upper_left, 2))
    pairs = jnp.stack([contract(pair_forms[leg_idx], kept[leg_idx], site_block) for leg_idx in range(4)], axis=1)
    summed = pairs[:, :, 0] + pairs[:, :, 1]
    scale = jnp.sqrt(lax.optimization_barrier(jnp.mean(summed * summed, axis=(2, 3), keepdims=True)) + epsilon)
    twisted = (pairs[:, :, 0] - pairs[:, :, 1]) / scale
    return ((summed / scale).reshape(site_count, 4, D * D), twisted.reshape(site_count, 4, D * D))

def route(values, edge_msgs):
    in_up = jnp.concatenate([edge_msgs[:1, :, 0], values[:-1, :, 2]], axis=0)
    in_down = jnp.concatenate([values[1:, :, 0], edge_msgs[-1:, :, 2]], axis=0)
    in_left = jnp.concatenate([edge_msgs[:, :1, 1], values[:, :-1, 3]], axis=1)
    in_right = jnp.concatenate([values[:, 1:, 1], edge_msgs[:, -1:, 3]], axis=1)
    return jnp.stack([in_up, in_left, in_down, in_right], axis=2)

def leg_weights(msg_sum, twist_sum):
    weight_zero = math.cosh(coupling_step)
    weight_one = math.sinh(coupling_step)
    cross_weight = math.sqrt(weight_zero * weight_one)
    y_top = ((weight_zero * msg_sum + cross_weight * twist_sum) / math.sqrt(2.0)).astype(jnp.bfloat16).astype(jnp.float32)
    bottom = ((cross_weight * twist_sum + weight_one * msg_sum) / math.sqrt(2.0)).astype(jnp.bfloat16).astype(jnp.float32)
    gram_mat = jnp.einsum('...ab,...ac->...bc', y_top, y_top, precision=precise) + jnp.einsum('...ab,...ac->...bc', bottom, bottom, precision=precise)
    identity = jnp.eye(D, dtype=jnp.float32)
    trace_sum = lax.optimization_barrier(jnp.sum(gram_mat * identity, axis=(-2, -1), keepdims=True)) + epsilon
    current = gram_mat / trace_sum
    inverse = jnp.broadcast_to(identity, gram_mat.shape)
    for sweep in range(NS_STEPS):
        factor = 1.5 * identity - 0.5 * jnp.matmul(inverse, current, precision=precise)
        current, inverse = (jnp.matmul(current, factor, precision=precise), jnp.matmul(factor, inverse, precision=precise))
    inverse = inverse.astype(jnp.bfloat16).astype(jnp.float32)
    root_trace = jnp.sqrt(trace_sum)
    q_top = jnp.matmul(y_top, inverse, precision=precise) / root_trace
    q_bottom = jnp.matmul(bottom, inverse, precision=precise) / root_trace
    first = math.sqrt(weight_zero) * q_top
    second = math.sqrt(weight_one) * q_bottom
    return jnp.stack([first + second, first - second], axis=-3)

def update_row(tensors, weights):
    site_count = tensors.shape[0]
    site_block = tensors.reshape(site_count, 2, D, D, D, D).astype(jnp.float32)
    gated = (math.cosh(field_step) * site_block + math.sinh(field_step) * site_block[:, ::-1]).astype(jnp.bfloat16)
    for leg_idx in range(4):
        gated = contract(gate_forms[leg_idx], gated, weights[:, leg_idx]).astype(jnp.bfloat16)
    return gated.reshape(site_count, 2, D ** 4)

def reference(site_tensors, msg_in):
    incoming = msg_in
    for sweep in range(ITERS):
        summed, twisted = lax.map(lambda row_data: outgoing(row_data[0], row_data[1]), (site_tensors, incoming))
        incoming = route(summed, msg_in)
    twisted_in = route(twisted, jnp.zeros_like(msg_in))
    shape_env = (ROWS, COLS, 4, D, D)
    weights = leg_weights((summed + incoming).reshape(shape_env), (twisted + twisted_in).reshape(shape_env))
    row_ids = jnp.arange(ROWS)[:, None, None]
    col_ids = jnp.arange(COLS)[None, :, None]
    leg_ids = jnp.arange(4)[None, None, :]
    at_edge = (leg_ids == 0) & (row_ids == 0) | (leg_ids == 2) & (row_ids == ROWS - 1) | (leg_ids == 1) & (col_ids == 0) | (leg_ids == 3) & (col_ids == COLS - 1)
    identity = jnp.eye(D, dtype=jnp.float32)
    weights = jnp.where(at_edge[:, :, :, None, None, None], identity, weights).astype(jnp.bfloat16)
    new_tensors = lax.map(lambda row_data: update_row(row_data[0], row_data[1]), (site_tensors, weights))
    return (new_tensors, incoming)
```

```python
import functools
import math

import jax
import jax.numpy as jnp
from jax import lax
from jax.experimental import pallas as pl
from jax.experimental.pallas import tpu as pltpu
from jax.sharding import PartitionSpec as P

ITERS = 2
NS_STEPS = 6
LANES = 128
EPSILON = 1e-06
COUPLING = 0.5
FIELD = 0.3
F32 = jnp.float32
BF16 = jnp.bfloat16
MESH = pl.DeviceIdType.MESH


def iota(shape, axis):
    return lax.broadcasted_iota(jnp.int32, shape, axis)


def dot(a, b):
    return jnp.dot(a, b, preferred_element_type=F32)


def dot_nt(a, b):
    return lax.dot_general(a, b, (((1,), (1,)), ((), ())), preferred_element_type=F32)


def dot_tn(a, b):
    return lax.dot_general(a, b, (((0,), (0,)), ((), ())), preferred_element_type=F32)


def parts(value, count):
    out = []
    for _ in range(count):
        piece = value.astype(BF16)
        out.append(piece)
        value = value - piece.astype(F32)
    return out


def select_dot(value, selector, count):
    total = None
    for piece in parts(value, count):
        term = dot(piece, selector)
        total = term if total is None else total + term
    return total


def dot3(a, b):
    (a_hi, a_lo), (b_hi, b_lo) = parts(a, 2), parts(b, 2)
    return dot(a_hi, b_hi) + (dot(a_hi, b_lo) + dot(a_lo, b_hi))


def one_hot(mask):
    return jnp.where(mask, 1.0, 0.0).astype(BF16)


def kernel(tiles, groups, cols, D, a_ref, msg_ref, out_ref, mout_ref,
           x_ref, xt_ref, ax_ref, kron_ref,
           send_up, send_down, send_side, recv_up, recv_down, recv_side,
           send_sem, recv_sem):
    tile = lax.axis_index("tile")
    group = lax.axis_index("group")
    DD = D * D
    shift = D.bit_length() - 1
    halves = DD // LANES
    mixed = 2 * halves
    rows = DD // mixed
    legs = 4 * cols
    wide = legs * D
    has_up = tile > 0
    has_down = tile < tiles - 1

    barrier = pltpu.get_barrier_semaphore()

    @pl.when(has_up)
    def _():
        pl.semaphore_signal(barrier, inc=1, device_id={"tile": tile - 1}, device_id_type=MESH)

    @pl.when(has_down)
    def _():
        pl.semaphore_signal(barrier, inc=1, device_id={"tile": tile + 1}, device_id_type=MESH)

    pl.semaphore_signal(barrier, inc=1, device_id={"group": 1 - group}, device_id_type=MESH)

    lane = iota((D, DD), 1)
    row = iota((D, DD), 0)
    major = one_hot((lane >> shift) == row)
    minor = one_hot((lane & (D - 1)) == row)
    both = jnp.concatenate([major, minor], axis=1)
    major_t = one_hot((iota((DD, D), 0) >> shift) == iota((DD, D), 1))
    minor_t = one_hot((iota((DD, D), 0) & (D - 1)) == iota((DD, D), 1))

    def permutation(out_axis):
        p, k = iota((DD, DD), out_axis), iota((DD, DD), 1 - out_axis)
        row_bits = rows.bit_length() - 1
        return one_hot(k == (p & (rows - 1)) * mixed + (p >> row_bits))

    unfold_mask = (lane >> shift) == row
    flat = msg_ref[...].reshape(legs, DD)
    spread = jnp.concatenate(
        [jnp.where(unfold_mask, flat[m : m + 1, :], 0.0) for m in range(legs)], axis=0
    )
    edge_all = select_dot(spread, minor_t, 3)
    edge = [edge_all[m * D : (m + 1) * D] for m in range(legs)]

    gather = permutation(0)
    for i in range(cols):
        for b in range(DD // rows):
            block = dot(gather, a_ref[i, b * DD : (b + 1) * DD, :]).astype(BF16)
            for g in range(mixed):
                x_ref[
                    i, g % 2, b * rows : (b + 1) * rows, (g // 2) * LANES : (g // 2 + 1) * LANES
                ] = block[g * rows : (g + 1) * rows]
        for s in range(2):
            xt_ref[i, s] = x_ref[i, s].T

    def build_kron(slot, first, second):
        for d in range(D):
            kron_ref[slot, d * D : (d + 1) * D, :] = (first[d : d + 1, :] * second).astype(BF16)

    def outgoing(incoming, last):
        stacked = jnp.concatenate([v.astype(BF16) for v in incoming], axis=0)
        spread = dot(stacked, both)

        def by_major(m):
            return spread[m * D : (m + 1) * D, :DD]

        def by_minor(m):
            return spread[m * D : (m + 1) * D, DD:]

        firsts, seconds = [], []
        for i in range(cols):
            for path in range(2):
                left, right = (x_ref, xt_ref) if path == 0 else (xt_ref, x_ref)
                far = i * 4 + 2 * (1 - path)
                near = i * 4 + 2 * path
                slot = i * 2 + path
                build_kron(slot, by_major(far), by_minor(far + 1))
                near_major, near_minor = by_major(near), by_minor(near + 1)
                pair = []
                for s in range(2):
                    y = dot(left[i, s], kron_ref[slot]).astype(BF16)
                    gram = dot(y, right[i, s])
                    first = jnp.concatenate(
                        [
                            jnp.sum(
                                gram[d * D : (d + 1) * D] * near_minor, axis=0, keepdims=True
                            )
                            for d in range(D)
                        ],
                        axis=0,
                    )
                    second = gram[:D] * near_major[0:1, :]
                    for d in range(1, D):
                        second = second + gram[d * D : (d + 1) * D] * near_major[d : d + 1, :]
                    pair.append((first, second))
                firsts.append((pair[0][0] + pair[1][0], pair[0][0] - pair[1][0]))
                seconds.append((pair[0][1] + pair[1][1], pair[0][1] - pair[1][1]))
        kinds = 2 if last else 1
        reduced = []
        for kind in range(kinds):
            by_first = select_dot(jnp.concatenate([f[kind] for f in firsts], axis=0), major_t, 2)
            by_second = select_dot(jnp.concatenate([f[kind] for f in seconds], axis=0), minor_t, 2)
            blocks = []
            for slot in range(2 * cols):
                blocks.append(by_first[slot * D : (slot + 1) * D])
                blocks.append(by_second[slot * D : (slot + 1) * D])
            reduced.append(blocks)
        scales = [
            jnp.sqrt(jnp.sum(v * v, axis=(0, 1), keepdims=True) / DD + EPSILON) for v in reduced[0]
        ]
        return [[v / r for v, r in zip(blocks, scales)] for blocks in reduced]

    def exchange(turn, values):
        kinds = len(values)
        width = kinds * cols * D

        def packed(leg):
            return jnp.concatenate([b[i * 4 + leg] for b in values for i in range(cols)], axis=1)

        up_src = send_up.at[turn]
        down_src = send_down.at[turn]
        side_src = send_side.at[turn]
        send_up[turn, :, :width] = packed(0)
        send_down[turn, :, :width] = packed(2)
        side_right = jnp.concatenate([b[(cols - 1) * 4 + 3] for b in values], axis=1)
        side_left = jnp.concatenate([b[1] for b in values], axis=1)
        send_side[turn, :, : kinds * D] = jnp.where(group == 0, side_right, side_left)

        def copy(src, dst, k, device):
            return pltpu.make_async_remote_copy(
                src_ref=src, dst_ref=dst.at[turn], send_sem=send_sem.at[turn, k],
                recv_sem=recv_sem.at[turn, k], device_id=device, device_id_type=MESH,
            )

        to_up = copy(up_src, recv_down, 0, {"tile": tile - 1})
        to_down = copy(down_src, recv_up, 1, {"tile": tile + 1})
        to_side = copy(side_src, recv_side, 2, {"group": 1 - group})

        @pl.when(has_up)
        def _():
            to_up.start()

        @pl.when(has_down)
        def _():
            to_down.start()

        to_side.start()
        return to_up, to_down, to_side

    def finish(turn, copies, values):
        to_up, to_down, to_side = copies
        kinds = len(values)
        width = kinds * cols * D

        def border(leg):
            blocks = [edge[i * 4 + leg] for i in range(cols)]
            if kinds == 2:
                blocks += [jnp.zeros((D, D), F32)] * cols
            return jnp.concatenate(blocks, axis=1)

        @pl.when(has_up)
        def _():
            to_up.wait_send()
            to_down.wait_recv()

        @pl.when(jnp.logical_not(has_up))
        def _():
            recv_up[turn, :, :width] = border(0)

        @pl.when(has_down)
        def _():
            to_down.wait_send()
            to_up.wait_recv()

        @pl.when(jnp.logical_not(has_down))
        def _():
            recv_down[turn, :, :width] = border(2)

        to_side.wait()
        from_up, from_down, from_side = recv_up[turn], recv_down[turn], recv_side[turn]
        routed = []
        for kind in range(kinds):
            blocks = []
            for i in range(cols):
                at = (kind * cols + i) * D
                side = from_side[:, kind * D : (kind + 1) * D]
                zero = jnp.zeros((D, D), F32)
                out_left = edge[i * 4 + 1] if kind == 0 else zero
                out_right = edge[i * 4 + 3] if kind == 0 else zero
                blocks.append(from_up[:, at : at + D])
                if i > 0:
                    blocks.append(values[kind][(i - 1) * 4 + 3])
                else:
                    blocks.append(jnp.where(group == 0, out_left, side))
                blocks.append(from_down[:, at : at + D])
                if i < cols - 1:
                    blocks.append(values[kind][(i + 1) * 4 + 1])
                else:
                    blocks.append(jnp.where(group == groups - 1, out_right, side))
            routed.append(blocks)
        return routed

    incoming = edge
    for turn in range(ITERS):
        last = turn == ITERS - 1
        values = outgoing(incoming, last)
        if turn == 0:
            inside = jnp.logical_and(has_up, has_down)

            @pl.when(inside)
            def _():
                pl.semaphore_wait(barrier, 3)

            @pl.when(jnp.logical_not(inside))
            def _():
                pl.semaphore_wait(barrier, 2)

        copies = exchange(turn, values)
        if last:
            for i in range(cols):
                a0, a1 = x_ref[i, 0].astype(F32), x_ref[i, 1].astype(F32)
                ch, sh = math.cosh(FIELD), math.sinh(FIELD)
                ax_ref[i, 0] = (ch * a0 + sh * a1).astype(BF16)
                ax_ref[i, 1] = (ch * a1 + sh * a0).astype(BF16)
        routed = finish(turn, copies, values)
        incoming = routed[0]

    stacked = jnp.concatenate(incoming, axis=0)
    spread = select_dot(stacked, minor, 3)
    flat_rows = [
        jnp.sum(
            jnp.where(unfold_mask, spread[m * D : (m + 1) * D], 0.0), axis=0, keepdims=True
        )
        for m in range(legs)
    ]
    mout_ref[...] = jnp.concatenate(flat_rows, axis=0).reshape(cols, 4, DD)

    g0, g1 = math.cosh(COUPLING), math.sinh(COUPLING)
    cross = math.sqrt(g0 * g1)
    root2 = math.sqrt(2.0)
    msg_sum = jnp.concatenate([o + n for o, n in zip(values[0], routed[0])], axis=1)
    twist_sum = jnp.concatenate([o + n for o, n in zip(values[1], routed[1])], axis=1)
    y_top = ((g0 * msg_sum + cross * twist_sum) / root2).astype(BF16)
    y_bot = ((cross * twist_sum + g1 * msg_sum) / root2).astype(BF16)
    y_both = jnp.concatenate([y_top, y_bot], axis=0)
    r_id, c_id = iota((wide, wide), 0), iota((wide, wide), 1)
    same = (r_id >> shift) == (c_id >> shift)
    eye = jnp.where(r_id == c_id, 1.0, 0.0).astype(F32)
    gram = jnp.where(same, dot_tn(y_both, y_both), 0.0)
    diag = jnp.sum(gram * eye, axis=0, keepdims=True)
    diag8 = jnp.broadcast_to(diag, (8, wide))
    trace = select_dot(diag8, one_hot(same), 3)[0:1] + EPSILON
    current = gram / trace
    inverse = eye
    for step in range(NS_STEPS):
        if step == 0:
            factor = 1.5 * eye - 0.5 * current
            inverse_next = factor
        else:
            factor = 1.5 * eye - 0.5 * dot3(inverse, current)
            inverse_next = dot3(factor, inverse)
        if step < NS_STEPS - 1:
            current = dot3(current, factor)
        inverse = inverse_next
    q_both = dot(y_both, inverse.astype(BF16)) / jnp.sqrt(trace)
    first = math.sqrt(g0) * q_both[:D]
    second = math.sqrt(g1) * q_both[D:]
    lane_w = iota((D, wide), 1)
    leg_of = (lane_w >> shift) & 3
    col_of = (lane_w >> (shift + 2)) + group * cols
    at_edge = (
        ((leg_of == 0) & (tile == 0))
        | ((leg_of == 2) & (tile == tiles - 1))
        | ((leg_of == 1) & (col_of == 0))
        | ((leg_of == 3) & (col_of == groups * cols - 1))
    )
    unit = jnp.where((lane_w & (D - 1)) == iota((D, wide), 0), 1.0, 0.0).astype(F32)
    scatter = permutation(1)
    spreads = []
    for weight in (first + second, first - second):
        weight = jnp.where(at_edge, unit, weight)
        spreads.append(dot(weight.T.astype(BF16), both))
    for i in range(cols):
        gated = []
        for s in range(2):
            w = spreads[s]
            m = i * 4
            build_kron(0 + 2 * s, w[(m + 2) * D : (m + 3) * D, :DD], w[(m + 3) * D : (m + 4) * D, DD:])
            build_kron(1 + 2 * s, w[m * D : (m + 1) * D, :DD], w[(m + 1) * D : (m + 2) * D, DD:])
            half = dot_nt(ax_ref[i, s], kron_ref[0 + 2 * s]).astype(BF16)
            gated.append(dot(kron_ref[1 + 2 * s], half).astype(BF16))
        for b in range(DD // rows):
            block = jnp.concatenate(
                [
                    gated[g % 2][
                        b * rows : (b + 1) * rows, (g // 2) * LANES : (g // 2 + 1) * LANES
                    ]
                    for g in range(mixed)
                ],
                axis=0,
            )
            out_ref[i, b * DD : (b + 1) * DD, :] = dot(scatter, block).astype(BF16)


def per_device(tiles, groups, site_tensors, msg_in):
    _, cols, _, size = site_tensors.shape
    DD = msg_in.shape[-1]
    D = math.isqrt(DD)
    chunks = size // LANES
    a = site_tensors.reshape(cols, 2, chunks, LANES).transpose(0, 2, 1, 3)
    a = a.reshape(cols, 2 * chunks, LANES)
    wide = 2 * cols * D
    vmem = pl.BlockSpec(memory_space=pltpu.VMEM)
    out, messages = pl.pallas_call(
        functools.partial(kernel, tiles, groups, cols, D),
        out_shape=(
            jax.ShapeDtypeStruct(a.shape, BF16),
            jax.ShapeDtypeStruct((cols, 4, DD), F32),
        ),
        in_specs=[vmem, vmem],
        out_specs=(vmem, vmem),
        scratch_shapes=[
            pltpu.VMEM((cols, 2, DD, DD), BF16),
            pltpu.VMEM((cols, 2, DD, DD), BF16),
            pltpu.VMEM((cols, 2, DD, DD), BF16),
            pltpu.VMEM((max(4, 2 * cols), DD, DD), BF16),
            pltpu.VMEM((ITERS, D, wide), F32),
            pltpu.VMEM((ITERS, D, wide), F32),
            pltpu.VMEM((ITERS, D, 2 * D), F32),
            pltpu.VMEM((ITERS, D, wide), F32),
            pltpu.VMEM((ITERS, D, wide), F32),
            pltpu.VMEM((ITERS, D, 2 * D), F32),
            pltpu.SemaphoreType.DMA((ITERS, 3)),
            pltpu.SemaphoreType.DMA((ITERS, 3)),
        ],
        compiler_params=pltpu.CompilerParams(collective_id=0, has_side_effects=True),
    )(a, msg_in[0])
    out = out.reshape(cols, chunks, 2, LANES).transpose(0, 2, 1, 3)
    return out.reshape(1, cols, 2, size), messages[None]


def solution(mesh):
    spec = P("tile", "group", None, None)
    return jax.shard_map(
        functools.partial(per_device, mesh.shape["tile"], mesh.shape["group"]),
        mesh=mesh, in_specs=(spec, spec), out_specs=(spec, spec), check_vma=False,
    )
```

```python
import functools
import math

import jax
import jax.numpy as jnp
from jax import lax
from jax.experimental import pallas as pl
from jax.experimental.pallas import tpu as pltpu
from jax.sharding import PartitionSpec as P

ITERS = 2
NS_STEPS = 6
LANES = 128
EPSILON = 1e-06
COUPLING = 0.5
FIELD = 0.3
F32 = jnp.float32
BF16 = jnp.bfloat16
MESH = pl.DeviceIdType.MESH


def iota(shape, axis):
    return lax.broadcasted_iota(jnp.int32, shape, axis)


def dot(a, b):
    return jnp.dot(a, b, preferred_element_type=F32)


def dot_nt(a, b):
    return lax.dot_general(a, b, (((1,), (1,)), ((), ())), preferred_element_type=F32)


def dot_tn(a, b):
    return lax.dot_general(a, b, (((0,), (0,)), ((), ())), preferred_element_type=F32)


def parts(value, count):
    out = []
    for _ in range(count):
        piece = value.astype(BF16)
        out.append(piece)
        value = value - piece.astype(F32)
    return out


def select_dot(value, selector, count):
    total = None
    for piece in parts(value, count):
        term = dot(piece, selector)
        total = term if total is None else total + term
    return total


def one_hot(mask):
    return jnp.where(mask, 1.0, 0.0).astype(BF16)


def build_kron(kron_ref, slot, first, second):
    D = first.shape[0]
    for d in range(D):
        kron_ref[slot, d * D : (d + 1) * D, :] = (first[d : d + 1, :] * second).astype(BF16)


def permutation(DD, rows, mixed, out_axis):
    p, k = iota((DD, DD), out_axis), iota((DD, DD), 1 - out_axis)
    row_bits = rows.bit_length() - 1
    return one_hot(k == (p & (rows - 1)) * mixed + (p >> row_bits))


def messages_kernel(tiles, groups, cols, D, a_ref, msg_ref, ax_ref, env_ref, mout_ref,
           x_ref, xt_ref, kron_ref, gram_ref,
           send_up, send_down, send_side, recv_up, recv_down, recv_side,
           send_sem, recv_sem):
    tile = lax.axis_index("tile")
    group = lax.axis_index("group")
    DD = D * D
    shift = D.bit_length() - 1
    halves = DD // LANES
    mixed = 2 * halves
    rows = DD // mixed
    legs = 4 * cols
    wide = legs * D
    has_up = tile > 0
    has_down = tile < tiles - 1

    barrier = pltpu.get_barrier_semaphore()

    @pl.when(has_up)
    def _():
        pl.semaphore_signal(barrier, inc=1, device_id={"tile": tile - 1}, device_id_type=MESH)

    @pl.when(has_down)
    def _():
        pl.semaphore_signal(barrier, inc=1, device_id={"tile": tile + 1}, device_id_type=MESH)

    pl.semaphore_signal(barrier, inc=1, device_id={"group": 1 - group}, device_id_type=MESH)

    lane = iota((D, DD), 1)
    row = iota((D, DD), 0)
    major = one_hot((lane >> shift) == row)
    minor = one_hot((lane & (D - 1)) == row)
    both = jnp.concatenate([major, minor], axis=1)
    major_t = one_hot((iota((DD, D), 0) >> shift) == iota((DD, D), 1))
    minor_t = one_hot((iota((DD, D), 0) & (D - 1)) == iota((DD, D), 1))

    unfold_mask = (lane >> shift) == row
    flat = msg_ref[...].reshape(legs, DD)
    spread = jnp.concatenate(
        [jnp.where(unfold_mask, flat[m : m + 1, :], 0.0) for m in range(legs)], axis=0
    )
    edge_all = select_dot(spread, minor_t, 3)
    edge = [edge_all[m * D : (m + 1) * D] for m in range(legs)]

    gather = permutation(DD, rows, mixed, 0)

    def unmix(i):
        for b in range(0, mixed, 2):
            pair = jnp.concatenate(
                [a_ref[i, b * DD : (b + 1) * DD, :], a_ref[i, (b + 1) * DD : (b + 2) * DD, :]],
                axis=1,
            )
            block = dot(gather, pair).astype(BF16)
            for c in range(2):
                for g in range(mixed):
                    x_ref[
                        i,
                        g % 2,
                        (b + c) * rows : (b + c + 1) * rows,
                        (g // 2) * LANES : (g // 2 + 1) * LANES,
                    ] = block[g * rows : (g + 1) * rows, c * LANES : (c + 1) * LANES]
        for s in range(2):
            xt_ref[i, s] = x_ref[i, s].T

    def reduce_major(gram, weight):
        total = gram[:D] * weight[0:1, :]
        for d in range(1, D):
            total = total + gram[d * D : (d + 1) * D] * weight[d : d + 1, :]
        return total

    def reduce_minor(gram, weight):
        return jnp.concatenate(
            [
                jnp.sum(gram[d * D : (d + 1) * D] * weight, axis=0, keepdims=True)
                for d in range(D)
            ],
            axis=0,
        )

    def kinds_of(totals):
        if len(totals) == 1:
            return totals
        return [totals[0] + totals[1], totals[0] - totals[1]]

    def outgoing(turn, incoming, last):
        stacked = jnp.concatenate([v.astype(BF16) for v in incoming], axis=0)
        spread = dot(stacked, both)
        kinds = 2 if last else 1

        def by_major(m):
            return spread[m * D : (m + 1) * D, :DD]

        def by_minor(m):
            return spread[m * D : (m + 1) * D, DD:]

        def normalised(totals, selector, slots):
            blocks = []
            for kind in range(kinds):
                rows_of = jnp.concatenate([t[kind] for t in totals], axis=0)
                blocks.append(select_dot(rows_of, selector, 2))
            out = {}
            for n, slot in enumerate(slots):
                own = [b[n * D : (n + 1) * D] for b in blocks]
                power = jnp.sum(own[0] * own[0], axis=(0, 1), keepdims=True) / DD
                scale = jnp.sqrt(power + EPSILON)
                out[slot] = [v / scale for v in own]
            return out

        firsts = []
        for i in range(cols):
            if turn == 0:
                unmix(i)
            for path in range(2):
                left, right = (x_ref, xt_ref) if path == 0 else (xt_ref, x_ref)
                far = i * 4 + 2 * (1 - path)
                near = i * 4 + 2 * path
                slot = i * 2 + path
                build_kron(kron_ref, slot, by_major(far), by_minor(far + 1))
                y = [dot(left[i, s], kron_ref[slot]).astype(BF16) for s in range(2)]
                if last:
                    grams = [dot(y[s], right[i, s]) for s in range(2)]
                else:
                    grams = [dot(y[0], right[i, 0]) + dot(y[1], right[i, 1])]
                for k, gram in enumerate(grams):
                    gram_ref[slot, k] = gram
                firsts.append(kinds_of([reduce_minor(g, by_minor(near + 1)) for g in grams]))

        def seconds(slots):
            totals = []
            for slot in slots:
                weight = by_major((slot // 2) * 4 + 2 * (slot % 2))
                totals.append(
                    kinds_of([reduce_major(gram_ref[slot, k], weight) for k in range(kinds)])
                )
            return normalised(totals, minor_t, slots)

        vertical = normalised(firsts, major_t, list(range(2 * cols)))
        ends = [0, 2 * cols - 1]
        sides = seconds(ends)

        def rest():
            others = [slot for slot in range(2 * cols) if slot not in ends]
            if others:
                sides.update(seconds(others))
            values = []
            for kind in range(kinds):
                blocks = []
                for slot in range(2 * cols):
                    blocks += [vertical[slot][kind], sides[slot][kind]]
                values.append(blocks)
            return values

        return vertical, sides, rest

    def exchange(turn, vertical, sides, kinds):
        width = kinds * cols * D

        def packed(path):
            return jnp.concatenate(
                [vertical[2 * i + path][k] for k in range(kinds) for i in range(cols)], axis=1
            )

        up_src = send_up.at[turn]
        down_src = send_down.at[turn]
        side_src = send_side.at[turn]
        send_up[turn, :, :width] = packed(0)
        send_down[turn, :, :width] = packed(1)
        side_right = jnp.concatenate(sides[2 * cols - 1], axis=1)
        side_left = jnp.concatenate(sides[0], axis=1)
        send_side[turn, :, : kinds * D] = jnp.where(group == 0, side_right, side_left)

        def copy(src, dst, k, device):
            return pltpu.make_async_remote_copy(
                src_ref=src, dst_ref=dst.at[turn], send_sem=send_sem.at[turn, k],
                recv_sem=recv_sem.at[turn, k], device_id=device, device_id_type=MESH,
            )

        to_up = copy(up_src, recv_down, 0, {"tile": tile - 1})
        to_down = copy(down_src, recv_up, 1, {"tile": tile + 1})
        to_side = copy(side_src, recv_side, 2, {"group": 1 - group})

        @pl.when(has_up)
        def _():
            to_up.start()

        @pl.when(has_down)
        def _():
            to_down.start()

        to_side.start()
        return to_up, to_down, to_side

    def finish(turn, copies, values):
        to_up, to_down, to_side = copies
        kinds = len(values)
        width = kinds * cols * D

        def border(leg):
            blocks = [edge[i * 4 + leg] for i in range(cols)]
            if kinds == 2:
                blocks += [jnp.zeros((D, D), F32)] * cols
            return jnp.concatenate(blocks, axis=1)

        @pl.when(has_up)
        def _():
            to_up.wait_send()
            to_down.wait_recv()

        @pl.when(jnp.logical_not(has_up))
        def _():
            recv_up[turn, :, :width] = border(0)

        @pl.when(has_down)
        def _():
            to_down.wait_send()
            to_up.wait_recv()

        @pl.when(jnp.logical_not(has_down))
        def _():
            recv_down[turn, :, :width] = border(2)

        to_side.wait()
        from_up, from_down, from_side = recv_up[turn], recv_down[turn], recv_side[turn]
        routed = []
        for kind in range(kinds):
            blocks = []
            for i in range(cols):
                at = (kind * cols + i) * D
                side = from_side[:, kind * D : (kind + 1) * D]
                zero = jnp.zeros((D, D), F32)
                out_left = edge[i * 4 + 1] if kind == 0 else zero
                out_right = edge[i * 4 + 3] if kind == 0 else zero
                blocks.append(from_up[:, at : at + D])
                if i > 0:
                    blocks.append(values[kind][(i - 1) * 4 + 3])
                else:
                    blocks.append(jnp.where(group == 0, out_left, side))
                blocks.append(from_down[:, at : at + D])
                if i < cols - 1:
                    blocks.append(values[kind][(i + 1) * 4 + 1])
                else:
                    blocks.append(jnp.where(group == groups - 1, out_right, side))
            routed.append(blocks)
        return routed

    incoming = edge
    for turn in range(ITERS):
        last = turn == ITERS - 1
        vertical, sides, rest = outgoing(turn, incoming, last)
        if turn == 0:
            inside = jnp.logical_and(has_up, has_down)

            @pl.when(inside)
            def _():
                pl.semaphore_wait(barrier, 3)

            @pl.when(jnp.logical_not(inside))
            def _():
                pl.semaphore_wait(barrier, 2)

        copies = exchange(turn, vertical, sides, 2 if last else 1)
        values = rest()
        if turn == 0:
            for i in range(cols):
                a0, a1 = x_ref[i, 0].astype(F32), x_ref[i, 1].astype(F32)
                ch, sh = math.cosh(FIELD), math.sinh(FIELD)
                ax_ref[i, 0] = (ch * a0 + sh * a1).astype(BF16)
                ax_ref[i, 1] = (ch * a1 + sh * a0).astype(BF16)
        routed = finish(turn, copies, values)
        incoming = routed[0]

    mout_ref[...] = jnp.concatenate(incoming, axis=0)
    env_ref[0] = jnp.concatenate([o + n for o, n in zip(values[0], routed[0])], axis=1)
    env_ref[1] = jnp.concatenate([o + n for o, n in zip(values[1], routed[1])], axis=1)
    lane_w = iota((D, wide), 1)
    leg_of = (lane_w >> shift) & 3
    col_of = (lane_w >> (shift + 2)) + group * cols
    at_edge = (
        ((leg_of == 0) & (tile == 0))
        | ((leg_of == 2) & (tile == tiles - 1))
        | ((leg_of == 1) & (col_of == 0))
        | ((leg_of == 3) & (col_of == groups * cols - 1))
    )
    env_ref[2] = jnp.where(at_edge, 1.0, 0.0).astype(F32)


def gates_kernel(cols, D, ax_ref, env_ref, in_ref, out_hbm, mout_ref,
                 kron_ref, out_ref, store_sem):
    DD = D * D
    shift = D.bit_length() - 1
    mixed = 2 * (DD // LANES)
    rows = DD // mixed
    legs = 4 * cols
    wide = legs * D
    lane = iota((D, DD), 1)
    row = iota((D, DD), 0)
    major = one_hot((lane >> shift) == row)
    minor = one_hot((lane & (D - 1)) == row)
    both = jnp.concatenate([major, minor], axis=1)

    spread = select_dot(in_ref[...], minor, 3)
    unfold_mask = (lane >> shift) == row
    flat_rows = [
        jnp.sum(
            jnp.where(unfold_mask, spread[m * D : (m + 1) * D], 0.0), axis=0, keepdims=True
        )
        for m in range(legs)
    ]
    mout_ref[...] = jnp.concatenate(flat_rows, axis=0).reshape(cols, 4, DD)

    g0, g1 = math.cosh(COUPLING), math.sinh(COUPLING)
    cross = math.sqrt(g0 * g1)
    root2 = math.sqrt(2.0)
    msg_sum, twist_sum = env_ref[0], env_ref[1]
    y_top = ((g0 * msg_sum + cross * twist_sum) / root2).astype(BF16)
    y_bot = ((cross * twist_sum + g1 * msg_sum) / root2).astype(BF16)
    y_both = jnp.concatenate([y_top, y_bot], axis=0)
    same = (iota((wide, wide), 0) >> shift) == (iota((wide, wide), 1) >> shift)
    same_bf = one_hot(same)
    lane_w = iota((D, wide), 1)
    unit = jnp.where((lane_w & (D - 1)) == iota((D, wide), 0), 1.0, 0.0).astype(F32)

    def diagonal(value):
        return jnp.concatenate([value] * legs, axis=0) * same_bf

    def times(left, right):
        count = left.shape[0]
        (l_hi, l_lo), (r_hi, r_lo) = parts(left, 2), parts(right, 2)
        main = dot(jnp.concatenate([l_hi, l_lo], axis=0), diagonal(r_hi))
        return main[:count] + (main[count:] + dot(l_hi, diagonal(r_lo)))

    full = jnp.where(same, dot_tn(y_both, y_both), 0.0)
    gram = full[:D]
    for m in range(1, legs):
        gram = gram + full[m * D : (m + 1) * D]
    diag = jnp.sum(gram * unit, axis=0, keepdims=True)
    trace = select_dot(jnp.broadcast_to(diag, (8, wide)), same_bf, 3)[0:1] + EPSILON
    current = gram / trace
    factor = 1.5 * unit - 0.5 * current
    inverse = factor
    current = times(current, factor)
    for step in range(1, NS_STEPS):
        factor = 1.5 * unit - 0.5 * times(inverse, current)
        if step < NS_STEPS - 1:
            stepped = times(jnp.concatenate([inverse, current], axis=0), factor)
            inverse, current = stepped[:D], stepped[D:]
        else:
            inverse = times(inverse, factor)
    q_both = dot(y_both, diagonal(inverse.astype(BF16))) / jnp.sqrt(trace)
    first = math.sqrt(g0) * q_both[:D]
    second = math.sqrt(g1) * q_both[D:]
    at_edge = env_ref[2] > 0.5
    scatter = permutation(DD, rows, mixed, 1)
    spreads = []
    for weight in (first + second, first - second):
        weight = jnp.where(at_edge, unit, weight)
        spreads.append(dot(weight.T.astype(BF16), both))
    stores = [
        pltpu.make_async_copy(out_ref.at[i], out_hbm.at[i], store_sem.at[i]) for i in range(cols)
    ]
    pairs = []
    for i in range(cols):
        m = i * 4
        gated = []
        for s in range(2):
            w = spreads[s]
            slot = (i * 2 + s) * 2
            build_kron(
                kron_ref, slot, w[(m + 2) * D : (m + 3) * D, :DD], w[(m + 3) * D : (m + 4) * D, DD:]
            )
            build_kron(
                kron_ref, slot + 1, w[m * D : (m + 1) * D, :DD], w[(m + 1) * D : (m + 2) * D, DD:]
            )
            half = dot_nt(ax_ref[i, s], kron_ref[slot]).astype(BF16)
            gated.append(dot(kron_ref[slot + 1], half).astype(BF16))
        pairs.append(gated)
    for i, gated in enumerate(pairs):
        for b in range(0, mixed, 2):
            block = jnp.concatenate(
                [
                    jnp.concatenate(
                        [
                            gated[g % 2][
                                (b + c) * rows : (b + c + 1) * rows,
                                (g // 2) * LANES : (g // 2 + 1) * LANES,
                            ]
                            for c in range(2)
                        ],
                        axis=1,
                    )
                    for g in range(mixed)
                ],
                axis=0,
            )
            done = dot(scatter, block).astype(BF16)
            for c in range(2):
                out_ref[i, (b + c) * DD : (b + c + 1) * DD, :] = done[
                    :, c * LANES : (c + 1) * LANES
                ]
        stores[i].start()
    for store in stores:
        store.wait()


def per_device(tiles, groups, site_tensors, msg_in):
    _, cols, _, size = site_tensors.shape
    DD = msg_in.shape[-1]
    D = math.isqrt(DD)
    chunks = size // LANES
    a = site_tensors.reshape(cols, 2, chunks, LANES).transpose(0, 2, 1, 3)
    a = a.reshape(cols, 2 * chunks, LANES)
    wide = 2 * cols * D
    legs = 4 * cols
    vmem = pl.BlockSpec(memory_space=pltpu.VMEM)
    anywhere = pl.BlockSpec(memory_space=pl.ANY)
    gated, env, stacked = pl.pallas_call(
        functools.partial(messages_kernel, tiles, groups, cols, D),
        out_shape=(
            jax.ShapeDtypeStruct((cols, 2, DD, DD), BF16),
            jax.ShapeDtypeStruct((3, D, legs * D), F32),
            jax.ShapeDtypeStruct((legs * D, D), F32),
        ),
        in_specs=[vmem, vmem],
        out_specs=(vmem, vmem, vmem),
        scratch_shapes=[
            pltpu.VMEM((cols, 2, DD, DD), BF16),
            pltpu.VMEM((cols, 2, DD, DD), BF16),
            pltpu.VMEM((2 * cols, DD, DD), BF16),
            pltpu.VMEM((2 * cols, 2, DD, DD), F32),
            pltpu.VMEM((ITERS, D, wide), F32),
            pltpu.VMEM((ITERS, D, wide), F32),
            pltpu.VMEM((ITERS, D, 2 * D), F32),
            pltpu.VMEM((ITERS, D, wide), F32),
            pltpu.VMEM((ITERS, D, wide), F32),
            pltpu.VMEM((ITERS, D, 2 * D), F32),
            pltpu.SemaphoreType.DMA((ITERS, 3)),
            pltpu.SemaphoreType.DMA((ITERS, 3)),
        ],
        compiler_params=pltpu.CompilerParams(
            collective_id=0, has_side_effects=True, vmem_limit_bytes=24 * 2**20
        ),
    )(a, msg_in[0])
    out, messages = pl.pallas_call(
        functools.partial(gates_kernel, cols, D),
        out_shape=(
            jax.ShapeDtypeStruct(a.shape, BF16),
            jax.ShapeDtypeStruct((cols, 4, DD), F32),
        ),
        in_specs=[vmem, vmem, vmem],
        out_specs=(anywhere, vmem),
        scratch_shapes=[
            pltpu.VMEM((4 * cols, DD, DD), BF16),
            pltpu.VMEM(a.shape, BF16),
            pltpu.SemaphoreType.DMA((cols,)),
        ],
        compiler_params=pltpu.CompilerParams(vmem_limit_bytes=24 * 2**20),
    )(gated, env, stacked)
    out = out.reshape(cols, chunks, 2, LANES).transpose(0, 2, 1, 3)
    return out.reshape(1, cols, 2, size), messages[None]


def solution(mesh):
    spec = P("tile", "group", None, None)
    return jax.shard_map(
        functools.partial(per_device, mesh.shape["tile"], mesh.shape["group"]),
        mesh=mesh, in_specs=(spec, spec), out_specs=(spec, spec), check_vma=False,
    )
```

```python
import functools
import math

import jax
import jax.numpy as jnp
from jax import lax
from jax.experimental import pallas as pl
from jax.experimental.pallas import tpu as pltpu
from jax.sharding import PartitionSpec as P

ITERS = 2
NS_STEPS = 6
LANES = 128
EPSILON = 1e-06
COUPLING = 0.5
FIELD = 0.3
F32 = jnp.float32
BF16 = jnp.bfloat16
MESH = pl.DeviceIdType.MESH


def iota(shape, axis):
    return lax.broadcasted_iota(jnp.int32, shape, axis)


def dot(a, b):
    return jnp.dot(a, b, preferred_element_type=F32)


def dot_nt(a, b):
    return lax.dot_general(a, b, (((1,), (1,)), ((), ())), preferred_element_type=F32)


def dot_tn(a, b):
    return lax.dot_general(a, b, (((0,), (0,)), ((), ())), preferred_element_type=F32)


def parts(value, count):
    out = []
    for _ in range(count):
        piece = value.astype(BF16)
        out.append(piece)
        value = value - piece.astype(F32)
    return out


def select_dot(value, selector, count):
    total = None
    for piece in parts(value, count):
        term = dot(piece, selector)
        total = term if total is None else total + term
    return total


def one_hot(mask):
    return jnp.where(mask, 1.0, 0.0).astype(BF16)


def build_kron(kron_ref, slot, first, second):
    D = first.shape[0]
    for d in range(D):
        kron_ref[slot, d * D : (d + 1) * D, :] = (first[d : d + 1, :] * second).astype(BF16)


def permutation(DD, rows, mixed, out_axis):
    p, k = iota((DD, DD), out_axis), iota((DD, DD), 1 - out_axis)
    row_bits = rows.bit_length() - 1
    return one_hot(k == (p & (rows - 1)) * mixed + (p >> row_bits))


def messages_kernel(tiles, groups, cols, D, a_ref, msg_ref, ax_ref, env_ref, mout_ref,
           x_ref, xt_ref, kron_ref, gram_ref,
           send_up, send_down, send_side, recv_up, recv_down, recv_side,
           send_sem, recv_sem):
    tile = lax.axis_index("tile")
    group = lax.axis_index("group")
    DD = D * D
    shift = D.bit_length() - 1
    halves = DD // LANES
    mixed = 2 * halves
    rows = DD // mixed
    legs = 4 * cols
    wide = legs * D
    has_up = tile > 0
    has_down = tile < tiles - 1

    barrier = pltpu.get_barrier_semaphore()

    @pl.when(has_up)
    def _():
        pl.semaphore_signal(barrier, inc=1, device_id={"tile": tile - 1}, device_id_type=MESH)

    @pl.when(has_down)
    def _():
        pl.semaphore_signal(barrier, inc=1, device_id={"tile": tile + 1}, device_id_type=MESH)

    pl.semaphore_signal(barrier, inc=1, device_id={"group": 1 - group}, device_id_type=MESH)

    lane = iota((D, DD), 1)
    row = iota((D, DD), 0)
    major = one_hot((lane >> shift) == row)
    minor = one_hot((lane & (D - 1)) == row)
    both = jnp.concatenate([major, minor], axis=1)
    major_t = one_hot((iota((DD, D), 0) >> shift) == iota((DD, D), 1))
    minor_t = one_hot((iota((DD, D), 0) & (D - 1)) == iota((DD, D), 1))

    unfold_mask = (lane >> shift) == row
    flat = msg_ref[...].reshape(legs, DD)
    spread = jnp.concatenate(
        [jnp.where(unfold_mask, flat[m : m + 1, :], 0.0) for m in range(legs)], axis=0
    )
    edge_all = select_dot(spread, minor_t, 3)
    edge = [edge_all[m * D : (m + 1) * D] for m in range(legs)]

    gather = permutation(DD, rows, mixed, 0)

    def unmix(i):
        for b in range(0, mixed, 2):
            pair = jnp.concatenate(
                [a_ref[i, b * DD : (b + 1) * DD, :], a_ref[i, (b + 1) * DD : (b + 2) * DD, :]],
                axis=1,
            )
            block = dot(gather, pair).astype(BF16)
            for c in range(2):
                for g in range(mixed):
                    x_ref[
                        i,
                        g % 2,
                        (b + c) * rows : (b + c + 1) * rows,
                        (g // 2) * LANES : (g // 2 + 1) * LANES,
                    ] = block[g * rows : (g + 1) * rows, c * LANES : (c + 1) * LANES]
        for s in range(2):
            xt_ref[i, s] = x_ref[i, s].T

    def reduce_major(gram, weight):
        total = gram[:D] * weight[0:1, :]
        for d in range(1, D):
            total = total + gram[d * D : (d + 1) * D] * weight[d : d + 1, :]
        return total

    def reduce_minor(gram, weight):
        return jnp.concatenate(
            [
                jnp.sum(gram[d * D : (d + 1) * D] * weight, axis=0, keepdims=True)
                for d in range(D)
            ],
            axis=0,
        )

    def kinds_of(totals):
        if len(totals) == 1:
            return totals
        return [totals[0] + totals[1], totals[0] - totals[1]]

    def outgoing(turn, incoming, last):
        stacked = jnp.concatenate([v.astype(BF16) for v in incoming], axis=0)
        spread = dot(stacked, both)
        kinds = 2 if last else 1

        def by_major(m):
            return spread[m * D : (m + 1) * D, :DD]

        def by_minor(m):
            return spread[m * D : (m + 1) * D, DD:]

        def normalised(totals, selector, slots):
            blocks = []
            for kind in range(kinds):
                rows_of = jnp.concatenate([t[kind] for t in totals], axis=0)
                blocks.append(select_dot(rows_of, selector, 2))
            out = {}
            for n, slot in enumerate(slots):
                own = [b[n * D : (n + 1) * D] for b in blocks]
                power = jnp.sum(own[0] * own[0], axis=(0, 1), keepdims=True) / DD
                scale = jnp.sqrt(power + EPSILON)
                out[slot] = [v / scale for v in own]
            return out

        firsts = []
        for i in range(cols):
            if turn == 0:
                unmix(i)
            for path in range(2):
                left, right = (x_ref, xt_ref) if path == 0 else (xt_ref, x_ref)
                far = i * 4 + 2 * (1 - path)
                near = i * 4 + 2 * path
                slot = i * 2 + path
                build_kron(kron_ref, slot, by_major(far), by_minor(far + 1))
                y = [dot(left[i, s], kron_ref[slot]).astype(BF16) for s in range(2)]
                if last:
                    grams = [dot(y[s], right[i, s]) for s in range(2)]
                else:
                    grams = [dot(y[0], right[i, 0]) + dot(y[1], right[i, 1])]
                for k, gram in enumerate(grams):
                    gram_ref[slot, k] = gram
                firsts.append(kinds_of([reduce_minor(g, by_minor(near + 1)) for g in grams]))

        def seconds(slots):
            totals = []
            for slot in slots:
                weight = by_major((slot // 2) * 4 + 2 * (slot % 2))
                totals.append(
                    kinds_of([reduce_major(gram_ref[slot, k], weight) for k in range(kinds)])
                )
            return normalised(totals, minor_t, slots)

        vertical = normalised(firsts, major_t, list(range(2 * cols)))
        ends = [0, 2 * cols - 1]
        sides = seconds(ends)

        def rest():
            others = [slot for slot in range(2 * cols) if slot not in ends]
            if others:
                sides.update(seconds(others))
            values = []
            for kind in range(kinds):
                blocks = []
                for slot in range(2 * cols):
                    blocks += [vertical[slot][kind], sides[slot][kind]]
                values.append(blocks)
            return values

        return vertical, sides, rest

    def exchange(turn, vertical, sides, kinds):
        width = kinds * cols * D

        def packed(path):
            return jnp.concatenate(
                [vertical[2 * i + path][k] for k in range(kinds) for i in range(cols)], axis=1
            )

        up_src = send_up.at[turn]
        down_src = send_down.at[turn]
        side_src = send_side.at[turn]
        send_up[turn, :, :width] = packed(0)
        send_down[turn, :, :width] = packed(1)
        side_right = jnp.concatenate(sides[2 * cols - 1], axis=1)
        side_left = jnp.concatenate(sides[0], axis=1)
        send_side[turn, :, : kinds * D] = jnp.where(group == 0, side_right, side_left)

        def copy(src, dst, k, device):
            return pltpu.make_async_remote_copy(
                src_ref=src, dst_ref=dst.at[turn], send_sem=send_sem.at[turn, k],
                recv_sem=recv_sem.at[turn, k], device_id=device, device_id_type=MESH,
            )

        to_up = copy(up_src, recv_down, 0, {"tile": tile - 1})
        to_down = copy(down_src, recv_up, 1, {"tile": tile + 1})
        to_side = copy(side_src, recv_side, 2, {"group": 1 - group})

        @pl.when(has_up)
        def _():
            to_up.start()

        @pl.when(has_down)
        def _():
            to_down.start()

        to_side.start()
        return to_up, to_down, to_side

    def finish(turn, copies, values):
        to_up, to_down, to_side = copies
        kinds = len(values)
        width = kinds * cols * D

        def border(leg):
            blocks = [edge[i * 4 + leg] for i in range(cols)]
            if kinds == 2:
                blocks += [jnp.zeros((D, D), F32)] * cols
            return jnp.concatenate(blocks, axis=1)

        @pl.when(has_up)
        def _():
            to_up.wait_send()
            to_down.wait_recv()

        @pl.when(jnp.logical_not(has_up))
        def _():
            recv_up[turn, :, :width] = border(0)

        @pl.when(has_down)
        def _():
            to_down.wait_send()
            to_up.wait_recv()

        @pl.when(jnp.logical_not(has_down))
        def _():
            recv_down[turn, :, :width] = border(2)

        to_side.wait()
        from_up, from_down, from_side = recv_up[turn], recv_down[turn], recv_side[turn]
        routed = []
        for kind in range(kinds):
            blocks = []
            for i in range(cols):
                at = (kind * cols + i) * D
                side = from_side[:, kind * D : (kind + 1) * D]
                zero = jnp.zeros((D, D), F32)
                out_left = edge[i * 4 + 1] if kind == 0 else zero
                out_right = edge[i * 4 + 3] if kind == 0 else zero
                blocks.append(from_up[:, at : at + D])
                if i > 0:
                    blocks.append(values[kind][(i - 1) * 4 + 3])
                else:
                    blocks.append(jnp.where(group == 0, out_left, side))
                blocks.append(from_down[:, at : at + D])
                if i < cols - 1:
                    blocks.append(values[kind][(i + 1) * 4 + 1])
                else:
                    blocks.append(jnp.where(group == groups - 1, out_right, side))
            routed.append(blocks)
        return routed

    incoming = edge
    for turn in range(ITERS):
        last = turn == ITERS - 1
        vertical, sides, rest = outgoing(turn, incoming, last)
        if turn == 0:
            inside = jnp.logical_and(has_up, has_down)

            @pl.when(inside)
            def _():
                pl.semaphore_wait(barrier, 3)

            @pl.when(jnp.logical_not(inside))
            def _():
                pl.semaphore_wait(barrier, 2)

        copies = exchange(turn, vertical, sides, 2 if last else 1)
        values = rest()
        if turn == 0:
            for i in range(cols):
                a0, a1 = x_ref[i, 0].astype(F32), x_ref[i, 1].astype(F32)
                ch, sh = math.cosh(FIELD), math.sinh(FIELD)
                ax_ref[i, 0] = (ch * a0 + sh * a1).astype(BF16)
                ax_ref[i, 1] = (ch * a1 + sh * a0).astype(BF16)
        routed = finish(turn, copies, values)
        incoming = routed[0]

    mout_ref[...] = jnp.concatenate(incoming, axis=0)
    env_ref[0] = jnp.concatenate([o + n for o, n in zip(values[0], routed[0])], axis=1)
    env_ref[1] = jnp.concatenate([o + n for o, n in zip(values[1], routed[1])], axis=1)
    lane_w = iota((D, wide), 1)
    leg_of = (lane_w >> shift) & 3
    col_of = (lane_w >> (shift + 2)) + group * cols
    at_edge = (
        ((leg_of == 0) & (tile == 0))
        | ((leg_of == 2) & (tile == tiles - 1))
        | ((leg_of == 1) & (col_of == 0))
        | ((leg_of == 3) & (col_of == groups * cols - 1))
    )
    env_ref[2] = jnp.where(at_edge, 1.0, 0.0).astype(F32)


def gates_kernel(cols, D, ax_ref, env_ref, in_ref, out_hbm, mout_hbm,
                 kron_ref, out_ref, mout_ref, store_sem):
    DD = D * D
    shift = D.bit_length() - 1
    mixed = 2 * (DD // LANES)
    rows = DD // mixed
    legs = 4 * cols
    wide = legs * D
    lane = iota((D, DD), 1)
    row = iota((D, DD), 0)
    major = one_hot((lane >> shift) == row)
    minor = one_hot((lane & (D - 1)) == row)
    both = jnp.concatenate([major, minor], axis=1)

    spread = select_dot(in_ref[...], minor, 3)
    unfold_mask = (lane >> shift) == row
    flat_rows = [
        jnp.sum(
            jnp.where(unfold_mask, spread[m * D : (m + 1) * D], 0.0), axis=0, keepdims=True
        )
        for m in range(legs)
    ]
    mout_ref[...] = jnp.concatenate(flat_rows, axis=0).reshape(cols, 4, DD)
    store_msg = pltpu.make_async_copy(mout_ref, mout_hbm, store_sem.at[cols])
    store_msg.start()

    g0, g1 = math.cosh(COUPLING), math.sinh(COUPLING)
    cross = math.sqrt(g0 * g1)
    root2 = math.sqrt(2.0)
    msg_sum, twist_sum = env_ref[0], env_ref[1]
    y_top = ((g0 * msg_sum + cross * twist_sum) / root2).astype(BF16)
    y_bot = ((cross * twist_sum + g1 * msg_sum) / root2).astype(BF16)
    y_both = jnp.concatenate([y_top, y_bot], axis=0)
    same = (iota((wide, wide), 0) >> shift) == (iota((wide, wide), 1) >> shift)
    same_bf = one_hot(same)
    lane_w = iota((D, wide), 1)
    unit = jnp.where((lane_w & (D - 1)) == iota((D, wide), 0), 1.0, 0.0).astype(F32)

    def diagonal(value):
        return jnp.concatenate([value] * legs, axis=0) * same_bf

    def times(left, right):
        count = left.shape[0]
        (l_hi, l_lo), (r_hi, r_lo) = parts(left, 2), parts(right, 2)
        main = dot(jnp.concatenate([l_hi, l_lo], axis=0), diagonal(r_hi))
        return main[:count] + (main[count:] + dot(l_hi, diagonal(r_lo)))

    full = jnp.where(same, dot_tn(y_both, y_both), 0.0)
    gram = full[:D]
    for m in range(1, legs):
        gram = gram + full[m * D : (m + 1) * D]
    diag = jnp.sum(gram * unit, axis=0, keepdims=True)
    trace = select_dot(jnp.broadcast_to(diag, (8, wide)), same_bf, 3)[0:1] + EPSILON
    current = gram / trace
    factor = 1.5 * unit - 0.5 * current
    inverse = factor
    current = times(current, factor)
    for step in range(1, NS_STEPS):
        factor = 1.5 * unit - 0.5 * times(inverse, current)
        if step < NS_STEPS - 1:
            stepped = times(jnp.concatenate([inverse, current], axis=0), factor)
            inverse, current = stepped[:D], stepped[D:]
        else:
            inverse = times(inverse, factor)
    q_both = dot(y_both, diagonal(inverse.astype(BF16))) / jnp.sqrt(trace)
    first = math.sqrt(g0) * q_both[:D]
    second = math.sqrt(g1) * q_both[D:]
    at_edge = env_ref[2] > 0.5
    scatter = permutation(DD, rows, mixed, 1)
    spreads = []
    for weight in (first + second, first - second):
        weight = jnp.where(at_edge, unit, weight)
        spreads.append(dot(weight.T.astype(BF16), both))
    stores = [
        pltpu.make_async_copy(out_ref.at[i], out_hbm.at[i], store_sem.at[i]) for i in range(cols)
    ]
    def gate(i):
        m = i * 4
        gated = []
        for s in range(2):
            w = spreads[s]
            slot = (i * 2 + s) * 2
            build_kron(
                kron_ref, slot, w[(m + 2) * D : (m + 3) * D, :DD], w[(m + 3) * D : (m + 4) * D, DD:]
            )
            build_kron(
                kron_ref, slot + 1, w[m * D : (m + 1) * D, :DD], w[(m + 1) * D : (m + 2) * D, DD:]
            )
            half = dot_nt(ax_ref[i, s], kron_ref[slot]).astype(BF16)
            gated.append(dot(kron_ref[slot + 1], half).astype(BF16))
        return gated

    def emit(i, gated):
        for b in range(0, mixed, 2):
            block = jnp.concatenate(
                [
                    jnp.concatenate(
                        [
                            gated[g % 2][
                                (b + c) * rows : (b + c + 1) * rows,
                                (g // 2) * LANES : (g // 2 + 1) * LANES,
                            ]
                            for c in range(2)
                        ],
                        axis=1,
                    )
                    for g in range(mixed)
                ],
                axis=0,
            )
            done = dot(scatter, block).astype(BF16)
            for c in range(2):
                out_ref[i, (b + c) * DD : (b + c + 1) * DD, :] = done[
                    :, c * LANES : (c + 1) * LANES
                ]
        stores[i].start()

    waiting = gate(0)
    for i in range(cols):
        following = gate(i + 1) if i + 1 < cols else None
        emit(i, waiting)
        waiting = following
    for store in stores + [store_msg]:
        store.wait()


def per_device(tiles, groups, site_tensors, msg_in):
    _, cols, _, size = site_tensors.shape
    DD = msg_in.shape[-1]
    D = math.isqrt(DD)
    chunks = size // LANES
    a = site_tensors.reshape(cols, 2, chunks, LANES).transpose(0, 2, 1, 3)
    a = a.reshape(cols, 2 * chunks, LANES)
    wide = 2 * cols * D
    legs = 4 * cols
    vmem = pl.BlockSpec(memory_space=pltpu.VMEM)
    hbm = pl.BlockSpec(memory_space=pltpu.HBM)
    gated, env, stacked = pl.pallas_call(
        functools.partial(messages_kernel, tiles, groups, cols, D),
        out_shape=(
            jax.ShapeDtypeStruct((cols, 2, DD, DD), BF16),
            jax.ShapeDtypeStruct((3, D, legs * D), F32),
            jax.ShapeDtypeStruct((legs * D, D), F32),
        ),
        in_specs=[vmem, vmem],
        out_specs=(vmem, vmem, vmem),
        scratch_shapes=[
            pltpu.VMEM((cols, 2, DD, DD), BF16),
            pltpu.VMEM((cols, 2, DD, DD), BF16),
            pltpu.VMEM((2 * cols, DD, DD), BF16),
            pltpu.VMEM((2 * cols, 2, DD, DD), F32),
            pltpu.VMEM((ITERS, D, wide), F32),
            pltpu.VMEM((ITERS, D, wide), F32),
            pltpu.VMEM((ITERS, D, 2 * D), F32),
            pltpu.VMEM((ITERS, D, wide), F32),
            pltpu.VMEM((ITERS, D, wide), F32),
            pltpu.VMEM((ITERS, D, 2 * D), F32),
            pltpu.SemaphoreType.DMA((ITERS, 3)),
            pltpu.SemaphoreType.DMA((ITERS, 3)),
        ],
        compiler_params=pltpu.CompilerParams(
            collective_id=0, has_side_effects=True, vmem_limit_bytes=24 * 2**20
        ),
    )(a, msg_in[0])
    out, messages = pl.pallas_call(
        functools.partial(gates_kernel, cols, D),
        out_shape=(
            jax.ShapeDtypeStruct(a.shape, BF16),
            jax.ShapeDtypeStruct((cols, 4, DD), F32),
        ),
        in_specs=[vmem, vmem, vmem],
        out_specs=(hbm, hbm),
        scratch_shapes=[
            pltpu.VMEM((4 * cols, DD, DD), BF16),
            pltpu.VMEM(a.shape, BF16),
            pltpu.VMEM((cols, 4, DD), F32),
            pltpu.SemaphoreType.DMA((cols + 1,)),
        ],
        compiler_params=pltpu.CompilerParams(vmem_limit_bytes=24 * 2**20),
    )(gated, env, stacked)
    out = out.reshape(cols, chunks, 2, LANES).transpose(0, 2, 1, 3)
    return out.reshape(1, cols, 2, size), messages[None]


def solution(mesh):
    spec = P("tile", "group", None, None)
    return jax.shard_map(
        functools.partial(per_device, mesh.shape["tile"], mesh.shape["group"]),
        mesh=mesh, in_specs=(spec, spec), out_specs=(spec, spec), check_vma=False,
    )
```

```python
import functools
import math

import jax
import jax.numpy as jnp
from jax import lax
from jax.experimental import pallas as pl
from jax.experimental.pallas import tpu as pltpu
from jax.sharding import PartitionSpec as P

ITERS = 2
NS_STEPS = 6
LANES = 128
EPSILON = 1e-06
COUPLING = 0.5
FIELD = 0.3
F32 = jnp.float32
BF16 = jnp.bfloat16
MESH = pl.DeviceIdType.MESH


def iota(shape, axis):
    return lax.broadcasted_iota(jnp.int32, shape, axis)


def dot(a, b):
    return jnp.dot(a, b, preferred_element_type=F32)


def dot_nt(a, b):
    return lax.dot_general(a, b, (((1,), (1,)), ((), ())), preferred_element_type=F32)


def dot_tn(a, b):
    return lax.dot_general(a, b, (((0,), (0,)), ((), ())), preferred_element_type=F32)


def parts(value, count):
    out = []
    for _ in range(count):
        piece = value.astype(BF16)
        out.append(piece)
        value = value - piece.astype(F32)
    return out


def select_dot(value, selector, count):
    total = None
    for piece in parts(value, count):
        term = dot(piece, selector)
        total = term if total is None else total + term
    return total


def one_hot(mask):
    return jnp.where(mask, 1.0, 0.0).astype(BF16)


def build_kron(kron_ref, slot, first, second):
    D = first.shape[0]
    for d in range(D):
        kron_ref[slot, d * D : (d + 1) * D, :] = (first[d : d + 1, :] * second).astype(BF16)


def permutation(DD, rows, mixed, out_axis):
    p, k = iota((DD, DD), out_axis), iota((DD, DD), 1 - out_axis)
    row_bits = rows.bit_length() - 1
    return one_hot(k == (p & (rows - 1)) * mixed + (p >> row_bits))


def messages_kernel(tiles, groups, cols, D, a_ref, msg_ref, ax_ref, env_ref, mout_ref,
           xx_ref, kron_ref, gram_ref,
           send_vert, send_side, recv_vert, recv_side,
           send_sem, recv_sem):
    tile = lax.axis_index("tile")
    group = lax.axis_index("group")
    DD = D * D
    shift = D.bit_length() - 1
    halves = DD // LANES
    mixed = 2 * halves
    rows = DD // mixed
    legs = 4 * cols
    wide = legs * D
    has_up = tile > 0
    has_down = tile < tiles - 1
    flip = tile % 2
    x_ref, xt_ref = xx_ref.at[0], xx_ref.at[1]

    barrier = pltpu.get_barrier_semaphore()

    @pl.when(has_up)
    def _():
        pl.semaphore_signal(barrier, inc=1, device_id={"tile": tile - 1}, device_id_type=MESH)

    @pl.when(has_down)
    def _():
        pl.semaphore_signal(barrier, inc=1, device_id={"tile": tile + 1}, device_id_type=MESH)

    pl.semaphore_signal(barrier, inc=1, device_id={"group": 1 - group}, device_id_type=MESH)

    lane = iota((D, DD), 1)
    row = iota((D, DD), 0)
    major = one_hot((lane >> shift) == row)
    minor = one_hot((lane & (D - 1)) == row)
    both = jnp.concatenate([major, minor], axis=1)
    major_t = one_hot((iota((DD, D), 0) >> shift) == iota((DD, D), 1))
    minor_t = one_hot((iota((DD, D), 0) & (D - 1)) == iota((DD, D), 1))

    unfold_mask = (lane >> shift) == row
    flat = msg_ref[...].reshape(legs, DD)
    spread = jnp.concatenate(
        [jnp.where(unfold_mask, flat[m : m + 1, :], 0.0) for m in range(legs)], axis=0
    )
    edge_all = select_dot(spread, minor_t, 3)
    edge = [edge_all[m * D : (m + 1) * D] for m in range(legs)]

    gather = permutation(DD, rows, mixed, 0)

    def unmix(i):
        for b in range(0, mixed, 2):
            pair = jnp.concatenate(
                [a_ref[i, b * DD : (b + 1) * DD, :], a_ref[i, (b + 1) * DD : (b + 2) * DD, :]],
                axis=1,
            )
            block = dot(gather, pair).astype(BF16)
            for c in range(2):
                for g in range(mixed):
                    x_ref[
                        i,
                        g % 2,
                        (b + c) * rows : (b + c + 1) * rows,
                        (g // 2) * LANES : (g // 2 + 1) * LANES,
                    ] = block[g * rows : (g + 1) * rows, c * LANES : (c + 1) * LANES]
        for s in range(2):
            xt_ref[i, s] = x_ref[i, s].T

    def reduce_major(gram, weight):
        total = gram[:D] * weight[0:1, :]
        for d in range(1, D):
            total = total + gram[d * D : (d + 1) * D] * weight[d : d + 1, :]
        return total

    def reduce_minor(gram, weight):
        return jnp.concatenate(
            [
                jnp.sum(gram[d * D : (d + 1) * D] * weight, axis=0, keepdims=True)
                for d in range(D)
            ],
            axis=0,
        )

    def kinds_of(totals):
        if len(totals) == 1:
            return totals
        return [totals[0] + totals[1], totals[0] - totals[1]]

    def outgoing(turn, incoming, last):
        stacked = jnp.concatenate([v.astype(BF16) for v in incoming], axis=0)
        spread = dot(stacked, both)
        kinds = 2 if last else 1

        def by_major(m):
            return spread[m * D : (m + 1) * D, :DD]

        def by_minor(m):
            return spread[m * D : (m + 1) * D, DD:]

        def normalised(totals, selector, slots):
            blocks = []
            for kind in range(kinds):
                rows_of = jnp.concatenate([t[kind] for t in totals], axis=0)
                blocks.append(select_dot(rows_of, selector, 2))
            out = {}
            for n, slot in enumerate(slots):
                own = [b[n * D : (n + 1) * D] for b in blocks]
                power = jnp.sum(own[0] * own[0], axis=(0, 1), keepdims=True) / DD
                scale = jnp.sqrt(power + EPSILON)
                out[slot] = [v / scale for v in own]
            return out

        def seconds(slots):
            totals = []
            for slot in slots:
                i, path = slot // 2, slot % 2
                held = i * 2 + (path + flip) % 2
                weight = by_major(i * 4 + 2 * path)
                totals.append(
                    kinds_of([reduce_major(gram_ref[held, k], weight) for k in range(kinds)])
                )
            return normalised(totals, minor_t, slots)

        phases, copies = [], []
        if turn == 0:
            for i in range(cols):
                unmix(i)
        for phase in range(2):
            path = (phase + flip) % 2
            upward = flip == phase
            firsts = []
            for i in range(cols):
                m = i * 4
                far_a = jnp.where(upward, by_major(m + 2), by_major(m))
                far_b = jnp.where(upward, by_minor(m + 3), by_minor(m + 1))
                near_b = jnp.where(upward, by_minor(m + 1), by_minor(m + 3))
                slot = i * 2 + phase
                build_kron(kron_ref, slot, far_a, far_b)
                y = [dot(xx_ref[path, i, s], kron_ref[slot]).astype(BF16) for s in range(2)]
                if last:
                    grams = [dot(y[s], xx_ref[1 - path, i, s]) for s in range(2)]
                else:
                    grams = [dot(y[0], xx_ref[1 - path, i, 0]) + dot(y[1], xx_ref[1 - path, i, 1])]
                for k, gram in enumerate(grams):
                    gram_ref[slot, k] = gram
                firsts.append(kinds_of([reduce_minor(g, near_b) for g in grams]))
            done = normalised(firsts, major_t, list(range(cols)))
            phases.append(done)
            if turn == 0 and phase == 0:
                enter()
            copies.append(send_vertical(turn, phase, done, kinds))

        ends = [0, 2 * cols - 1]
        sides = seconds(ends)
        vertical = {}
        for i in range(cols):
            for path in range(2):
                vertical[2 * i + path] = [
                    jnp.where(flip == 0, u, v)
                    for u, v in zip(phases[path][i], phases[1 - path][i])
                ]

        def rest():
            others = [slot for slot in range(2 * cols) if slot not in ends]
            if others:
                sides.update(seconds(others))
            values = []
            for kind in range(kinds):
                blocks = []
                for slot in range(2 * cols):
                    blocks += [vertical[slot][kind], sides[slot][kind]]
                values.append(blocks)
            return values

        return copies, sides, rest

    def enter():
        inside = jnp.logical_and(has_up, has_down)

        @pl.when(inside)
        def _():
            pl.semaphore_wait(barrier, 3)

        @pl.when(jnp.logical_not(inside))
        def _():
            pl.semaphore_wait(barrier, 2)

    def vertical_copy(turn, phase, slot, target):
        return pltpu.make_async_remote_copy(
            src_ref=send_vert.at[turn, phase], dst_ref=recv_vert.at[turn, slot],
            send_sem=send_sem.at[turn, phase], recv_sem=recv_sem.at[turn, slot],
            device_id={"tile": target}, device_id_type=MESH,
        )

    def send_vertical(turn, phase, done, kinds):
        send_vert[turn, phase, :, : kinds * cols * D] = jnp.concatenate(
            [done[i][k] for k in range(kinds) for i in range(cols)], axis=1
        )
        path = (phase + flip) % 2
        exists = jnp.where(flip == phase, tile, tiles - 1 - tile) > 0
        copy = vertical_copy(turn, phase, 1 - path, tile - 1 + 2 * path)

        @pl.when(exists)
        def _():
            copy.start()

        return copy, exists

    def exchange(turn, sides, kinds):
        side_right = jnp.concatenate(sides[2 * cols - 1], axis=1)
        side_left = jnp.concatenate(sides[0], axis=1)
        send_side[turn, :, : kinds * D] = jnp.where(group == 0, side_right, side_left)
        to_side = pltpu.make_async_remote_copy(
            src_ref=send_side.at[turn], dst_ref=recv_side.at[turn],
            send_sem=send_sem.at[turn, 2], recv_sem=recv_sem.at[turn, 2],
            device_id={"group": 1 - group}, device_id_type=MESH,
        )
        to_side.start()
        return to_side

    def finish(turn, copies, to_side, values):
        kinds = len(values)
        width = kinds * cols * D

        def border(leg):
            blocks = [edge[i * 4 + leg] for i in range(cols)]
            if kinds == 2:
                blocks += [jnp.zeros((D, D), F32)] * cols
            return jnp.concatenate(blocks, axis=1)

        for copy, exists in copies:
            @pl.when(exists)
            def _():
                copy.wait_send()

        for slot, present, leg, target in (
            (0, has_up, 0, tile - 1), (1, has_down, 2, tile + 1)
        ):
            @pl.when(present)
            def _():
                vertical_copy(turn, 0, slot, target).wait_recv()

            @pl.when(jnp.logical_not(present))
            def _():
                recv_vert[turn, slot, :, :width] = border(leg)

        to_side.wait()
        from_up, from_down, from_side = recv_vert[turn, 0], recv_vert[turn, 1], recv_side[turn]
        routed = []
        for kind in range(kinds):
            blocks = []
            for i in range(cols):
                at = (kind * cols + i) * D
                side = from_side[:, kind * D : (kind + 1) * D]
                zero = jnp.zeros((D, D), F32)
                out_left = edge[i * 4 + 1] if kind == 0 else zero
                out_right = edge[i * 4 + 3] if kind == 0 else zero
                blocks.append(from_up[:, at : at + D])
                if i > 0:
                    blocks.append(values[kind][(i - 1) * 4 + 3])
                else:
                    blocks.append(jnp.where(group == 0, out_left, side))
                blocks.append(from_down[:, at : at + D])
                if i < cols - 1:
                    blocks.append(values[kind][(i + 1) * 4 + 1])
                else:
                    blocks.append(jnp.where(group == groups - 1, out_right, side))
            routed.append(blocks)
        return routed

    incoming = edge
    for turn in range(ITERS):
        last = turn == ITERS - 1
        copies, sides, rest = outgoing(turn, incoming, last)
        to_side = exchange(turn, sides, 2 if last else 1)
        values = rest()
        if turn == 0:
            for i in range(cols):
                a0, a1 = x_ref[i, 0].astype(F32), x_ref[i, 1].astype(F32)
                ch, sh = math.cosh(FIELD), math.sinh(FIELD)
                ax_ref[i, 0] = (ch * a0 + sh * a1).astype(BF16)
                ax_ref[i, 1] = (ch * a1 + sh * a0).astype(BF16)
        routed = finish(turn, copies, to_side, values)
        incoming = routed[0]

    mout_ref[...] = jnp.concatenate(incoming, axis=0)
    env_ref[0] = jnp.concatenate([o + n for o, n in zip(values[0], routed[0])], axis=1)
    env_ref[1] = jnp.concatenate([o + n for o, n in zip(values[1], routed[1])], axis=1)
    lane_w = iota((D, wide), 1)
    leg_of = (lane_w >> shift) & 3
    col_of = (lane_w >> (shift + 2)) + group * cols
    at_edge = (
        ((leg_of == 0) & (tile == 0))
        | ((leg_of == 2) & (tile == tiles - 1))
        | ((leg_of == 1) & (col_of == 0))
        | ((leg_of == 3) & (col_of == groups * cols - 1))
    )
    env_ref[2] = jnp.where(at_edge, 1.0, 0.0).astype(F32)


def gates_kernel(cols, D, ax_ref, env_ref, in_ref, out_hbm, mout_hbm,
                 kron_ref, out_ref, mout_ref, store_sem):
    DD = D * D
    shift = D.bit_length() - 1
    mixed = 2 * (DD // LANES)
    rows = DD // mixed
    legs = 4 * cols
    wide = legs * D
    lane = iota((D, DD), 1)
    row = iota((D, DD), 0)
    major = one_hot((lane >> shift) == row)
    minor = one_hot((lane & (D - 1)) == row)
    both = jnp.concatenate([major, minor], axis=1)

    spread = select_dot(in_ref[...], minor, 3)
    unfold_mask = (lane >> shift) == row
    flat_rows = [
        jnp.sum(
            jnp.where(unfold_mask, spread[m * D : (m + 1) * D], 0.0), axis=0, keepdims=True
        )
        for m in range(legs)
    ]
    mout_ref[...] = jnp.concatenate(flat_rows, axis=0).reshape(cols, 4, DD)
    store_msg = pltpu.make_async_copy(mout_ref, mout_hbm, store_sem.at[cols])
    store_msg.start()

    g0, g1 = math.cosh(COUPLING), math.sinh(COUPLING)
    cross = math.sqrt(g0 * g1)
    root2 = math.sqrt(2.0)
    msg_sum, twist_sum = env_ref[0], env_ref[1]
    y_top = ((g0 * msg_sum + cross * twist_sum) / root2).astype(BF16)
    y_bot = ((cross * twist_sum + g1 * msg_sum) / root2).astype(BF16)
    y_both = jnp.concatenate([y_top, y_bot], axis=0)
    same = (iota((wide, wide), 0) >> shift) == (iota((wide, wide), 1) >> shift)
    same_bf = one_hot(same)
    lane_w = iota((D, wide), 1)
    unit = jnp.where((lane_w & (D - 1)) == iota((D, wide), 0), 1.0, 0.0).astype(F32)

    def diagonal(value):
        return jnp.concatenate([value] * legs, axis=0) * same_bf

    def times(left, right):
        count = left.shape[0]
        (l_hi, l_lo), (r_hi, r_lo) = parts(left, 2), parts(right, 2)
        main = dot(jnp.concatenate([l_hi, l_lo], axis=0), diagonal(r_hi))
        return main[:count] + (main[count:] + dot(l_hi, diagonal(r_lo)))

    full = jnp.where(same, dot_tn(y_both, y_both), 0.0)
    gram = full[:D]
    for m in range(1, legs):
        gram = gram + full[m * D : (m + 1) * D]
    diag = jnp.sum(gram * unit, axis=0, keepdims=True)
    trace = select_dot(jnp.broadcast_to(diag, (8, wide)), same_bf, 3)[0:1] + EPSILON
    current = gram / trace
    factor = 1.5 * unit - 0.5 * current
    inverse = factor
    current = times(current, factor)
    for step in range(1, NS_STEPS):
        factor = 1.5 * unit - 0.5 * times(inverse, current)
        if step < NS_STEPS - 1:
            stepped = times(jnp.concatenate([inverse, current], axis=0), factor)
            inverse, current = stepped[:D], stepped[D:]
        else:
            inverse = times(inverse, factor)
    q_both = dot(y_both, diagonal(inverse.astype(BF16))) / jnp.sqrt(trace)
    first = math.sqrt(g0) * q_both[:D]
    second = math.sqrt(g1) * q_both[D:]
    at_edge = env_ref[2] > 0.5
    scatter = permutation(DD, rows, mixed, 1)
    spreads = []
    for weight in (first + second, first - second):
        weight = jnp.where(at_edge, unit, weight)
        spreads.append(dot(weight.T.astype(BF16), both))
    stores = [
        pltpu.make_async_copy(out_ref.at[i], out_hbm.at[i], store_sem.at[i]) for i in range(cols)
    ]
    def gate(i):
        m = i * 4
        gated = []
        for s in range(2):
            w = spreads[s]
            slot = (i * 2 + s) * 2
            build_kron(
                kron_ref, slot, w[(m + 2) * D : (m + 3) * D, :DD], w[(m + 3) * D : (m + 4) * D, DD:]
            )
            build_kron(
                kron_ref, slot + 1, w[m * D : (m + 1) * D, :DD], w[(m + 1) * D : (m + 2) * D, DD:]
            )
            half = dot_nt(ax_ref[i, s], kron_ref[slot]).astype(BF16)
            gated.append(dot(kron_ref[slot + 1], half).astype(BF16))
        return gated

    def emit(i, gated):
        for b in range(0, mixed, 2):
            block = jnp.concatenate(
                [
                    jnp.concatenate(
                        [
                            gated[g % 2][
                                (b + c) * rows : (b + c + 1) * rows,
                                (g // 2) * LANES : (g // 2 + 1) * LANES,
                            ]
                            for c in range(2)
                        ],
                        axis=1,
                    )
                    for g in range(mixed)
                ],
                axis=0,
            )
            done = dot(scatter, block).astype(BF16)
            for c in range(2):
                out_ref[i, (b + c) * DD : (b + c + 1) * DD, :] = done[
                    :, c * LANES : (c + 1) * LANES
                ]
        stores[i].start()

    waiting = gate(0)
    for i in range(cols):
        following = gate(i + 1) if i + 1 < cols else None
        emit(i, waiting)
        waiting = following
    for store in stores + [store_msg]:
        store.wait()


def per_device(tiles, groups, site_tensors, msg_in):
    _, cols, _, size = site_tensors.shape
    DD = msg_in.shape[-1]
    D = math.isqrt(DD)
    chunks = size // LANES
    a = site_tensors.reshape(cols, 2, chunks, LANES).transpose(0, 2, 1, 3)
    a = a.reshape(cols, 2 * chunks, LANES)
    wide = 2 * cols * D
    legs = 4 * cols
    vmem = pl.BlockSpec(memory_space=pltpu.VMEM)
    hbm = pl.BlockSpec(memory_space=pltpu.HBM)
    gated, env, stacked = pl.pallas_call(
        functools.partial(messages_kernel, tiles, groups, cols, D),
        out_shape=(
            jax.ShapeDtypeStruct((cols, 2, DD, DD), BF16),
            jax.ShapeDtypeStruct((3, D, legs * D), F32),
            jax.ShapeDtypeStruct((legs * D, D), F32),
        ),
        in_specs=[vmem, vmem],
        out_specs=(vmem, vmem, vmem),
        scratch_shapes=[
            pltpu.VMEM((2, cols, 2, DD, DD), BF16),
            pltpu.VMEM((2 * cols, DD, DD), BF16),
            pltpu.VMEM((2 * cols, 2, DD, DD), F32),
            pltpu.VMEM((ITERS, 2, D, wide), F32),
            pltpu.VMEM((ITERS, D, 2 * D), F32),
            pltpu.VMEM((ITERS, 2, D, wide), F32),
            pltpu.VMEM((ITERS, D, 2 * D), F32),
            pltpu.SemaphoreType.DMA((ITERS, 3)),
            pltpu.SemaphoreType.DMA((ITERS, 3)),
        ],
        compiler_params=pltpu.CompilerParams(
            collective_id=0, has_side_effects=True, vmem_limit_bytes=24 * 2**20
        ),
    )(a, msg_in[0])
    out, messages = pl.pallas_call(
        functools.partial(gates_kernel, cols, D),
        out_shape=(
            jax.ShapeDtypeStruct(a.shape, BF16),
            jax.ShapeDtypeStruct((cols, 4, DD), F32),
        ),
        in_specs=[vmem, vmem, vmem],
        out_specs=(hbm, hbm),
        scratch_shapes=[
            pltpu.VMEM((4 * cols, DD, DD), BF16),
            pltpu.VMEM(a.shape, BF16),
            pltpu.VMEM((cols, 4, DD), F32),
            pltpu.SemaphoreType.DMA((cols + 1,)),
        ],
        compiler_params=pltpu.CompilerParams(vmem_limit_bytes=24 * 2**20),
    )(gated, env, stacked)
    out = out.reshape(cols, chunks, 2, LANES).transpose(0, 2, 1, 3)
    return out.reshape(1, cols, 2, size), messages[None]


def solution(mesh):
    spec = P("tile", "group", None, None)
    return jax.shard_map(
        functools.partial(per_device, mesh.shape["tile"], mesh.shape["group"]),
        mesh=mesh, in_specs=(spec, spec), out_specs=(spec, spec), check_vma=False,
    )
```
